32 devices in a mesh: parts: 2 (over y), wide: 4 (over z), narrow: 4 (over x, core).
Axes of the slice: x: 2, y: 2, z: 4, core: 2. Of those that a mesh axis runs over, the one named last changes fastest.
Arguments:
- embeddings: bfloat16 [8192, 1024], P(('parts', 'wide', 'narrow')), parts along dimension 0, may hold values from -6 to 6
- cluster_id: int32 [8192], P(('parts', 'wide', 'narrow')), parts along dimension 0, may hold values from 0 to 63, as said below
- order_index: int32 [8192], P(('parts', 'wide', 'narrow')), parts along dimension 0, may hold values from 0 to 2047, as said below
Outputs:
- nearest: float32 [8192], P(('parts', 'wide', 'narrow')), parts along dimension 0
The draws below stay inside these ranges and needn't reach their ends.
There are 2 independent parts, one for each index of `parts`. The reference program is written for one: setup_inputs(seed, part) draws one part's arguments, and reference() takes and returns one part's arrays. A program takes and returns all parts, laid end to end along the dimension named above; each array names one. Nothing has to cross between parts.
Inputs may be any that keep to these rules, and one draw needn't show every extreme that they name: `cluster_id`: cluster c belongs to owner c // 16 of wide; among the members held by one device at most 128 belong to clusters of one owner, and in every draw one owner gets exactly 128 from every device. `order_index`: the members of each cluster carry the distinct numbers 0, 1, 2, ... up to its size less one; in every draw some cluster holds 4 * 4 * 128 members.
All inputs are finite; a program needn't handle non-finite values.
Results may differ from the reference program's by a relative error of at most 0.00099.
Values may be sent and summed in bfloat16 or wider, within the bound.
A program may use at most 64 MiB of HBM per device.

```python
import math
import jax
import jax.numpy as jnp
from jax import lax

D = 1024
CPO = 16
M_DEV = 256
CAP = 128
MEMBERS = 4096
N_WIDE = 4
N_NARROW = 4


def members_layout(key):
    base = jax.random.fold_in(key, 11)
    k_full, k_perm, k_mix, k_first, k_second, k_turn, k_rank = jax.random.split(base, 7)
    devices = N_WIDE * N_NARROW
    slots = N_WIDE * CAP
    total = devices * M_DEV
    full_owner = jax.random.randint(k_full, (), 0, N_WIDE)
    slot_owner = jnp.arange(slots, dtype=jnp.int32) // CAP
    perms = jax.vmap(lambda k: jax.random.permutation(k, slots))(jax.random.split(k_perm, devices))
    score = perms.astype(jnp.int32) - jnp.where(slot_owner == full_owner, slots, 0).astype(jnp.int32)[None, :]
    chosen = jnp.argsort(score, axis=1)[:, :M_DEV]
    mixing = jax.vmap(lambda k: jax.random.permutation(k, M_DEV))(jax.random.split(k_mix, devices))
    chosen = jnp.take_along_axis(chosen, mixing, axis=1)
    owner = (chosen // CAP).reshape(total).astype(jnp.int32)
    first = jax.random.randint(k_first, (total,), 0, CPO)
    second = jax.random.randint(k_second, (total,), 0, CPO)
    turn = jax.random.randint(k_turn, (N_WIDE,), 0, CPO)
    spread = (first * second // CPO + turn[owner]) % CPO
    local = jnp.where(owner == full_owner, turn[owner], spread)
    cluster = (owner * CPO + local).astype(jnp.int32)
    ranks = jax.random.permutation(k_rank, total).astype(jnp.int32)
    sort_key = cluster * total + ranks
    index = jnp.argsort(sort_key)
    position = jnp.zeros((total,), jnp.int32).at[index].set(jnp.arange(total, dtype=jnp.int32))
    counts = jax.ops.segment_sum(jnp.ones((total,), jnp.int32), cluster, num_segments=N_WIDE * CPO)
    starts = jnp.cumsum(counts) - counts
    order = position - starts[cluster]
    return (cluster, order.astype(jnp.int32))


def draw_cluster_id(key, part):
    return members_layout(key)[0]


def draw_order_index(key, part):
    return members_layout(key)[1]


def block_scale(key, dims, shards, least, top_value):
    factor_of, own = 1.0, jax.random.fold_in(key, 6)
    for dim, parts in shards:
        heights = jnp.exp(jax.random.uniform(jax.random.fold_in(own, dim), (parts,), jnp.float32, least / len(shards), top_value / len(shards)))
        factor_of = factor_of * jnp.repeat(heights, dims[dim] // parts).reshape([-1 if axis == dim else 1 for axis in range(len(dims))])
    return factor_of


def gaussian(rng, dims, deviation, limit, pieces=(), kind=jnp.bfloat16):
    array = jax.random.normal(rng, dims, jnp.float32) * deviation
    if len(pieces) > 0:
        array = block_scale(rng, dims, pieces, -0.22, 0.18) * array
    return jnp.clip(array, min=-limit, max=limit).astype(kind)


def setup_inputs(seed: int = 0, part: int = 0) -> dict:
    splits = jax.random.split(jax.random.key(seed), 4)
    part_keys = jax.random.split(jax.random.fold_in(splits[3], part), 4)
    embeddings = gaussian(part_keys[0], (MEMBERS, D), 1.0, 6.0, ((0, 16),))
    cluster_id = draw_cluster_id(jax.random.fold_in(jax.random.fold_in(splits[3], part), 71), part)
    order_index = draw_order_index(jax.random.fold_in(jax.random.fold_in(splits[3], part), 71), part)
    return {"embeddings": embeddings, "cluster_id": cluster_id, "order_index": order_index}


def reference(embeddings, cluster_id, order_index):
    values = embeddings.astype(jnp.float32)
    unit = (values * lax.rsqrt(lax.optimization_barrier(jnp.sum(values * values, axis=1, keepdims=True)) + 1e-06)).astype(jnp.bfloat16)
    total = unit.shape[0]
    width = unit.shape[1]
    window = N_WIDE * N_NARROW * (2 * M_DEV // N_WIDE)
    block = math.gcd(total, 512)
    sort_key = cluster_id * total + order_index
    perm = jnp.argsort(sort_key).astype(jnp.int32)
    sorted_rows = unit[perm].astype(jnp.float32)
    sorted_cl = cluster_id[perm]
    sorted_or = order_index[perm]
    padded_rows = jnp.concatenate([jnp.zeros((window, width), jnp.float32), sorted_rows], axis=0)
    padded_cl = jnp.concatenate([jnp.full((window,), -1, jnp.int32), sorted_cl], axis=0)
    padded_or = jnp.concatenate([jnp.zeros((window,), jnp.int32), sorted_or], axis=0)

    def one_block(index):
        start = (index * block).astype(jnp.int32)
        query = lax.dynamic_slice_in_dim(sorted_rows, start, block, 0)
        query_cl = lax.dynamic_slice_in_dim(sorted_cl, start, block, 0)
        query_or = lax.dynamic_slice_in_dim(sorted_or, start, block, 0)
        keys = lax.dynamic_slice_in_dim(padded_rows, start, window + block, 0)
        keys_cl = lax.dynamic_slice_in_dim(padded_cl, start, window + block, 0)
        keys_or = lax.dynamic_slice_in_dim(padded_or, start, window + block, 0)
        inner = jnp.dot(query, keys.T, precision=lax.Precision.HIGHEST)
        allowed = (keys_cl[None, :] == query_cl[:, None]) & (keys_or[None, :] < query_or[:, None])
        return lax.optimization_barrier(jnp.max(jnp.where(allowed, inner, -1.0), axis=1))
    found = lax.map(one_block, jnp.arange(total // block, dtype=jnp.int32)).reshape(total)
    return jnp.zeros((total,), found.dtype).at[perm].set(found)
```

```python
import jax
import jax.numpy as jnp
from jax import lax
from jax.experimental import pallas as pl
from jax.experimental.pallas import tpu as pltpu
from jax.sharding import PartitionSpec as P

CPO = 16


def shifted(shard, axis, by):
    count = lax.axis_size(axis)
    return lax.ppermute(shard, axis, [(i, (i + by) % count) for i in range(count)])


def pair_inner(left, right):
    return lax.dot_general(
        left, right, (((1,), (1,)), ((), ())), preferred_element_type=jnp.float32
    )


def per_device(embeddings, cluster_id, order_index):
    wide_size = lax.axis_size("wide")
    rows = embeddings.shape[0]
    width = embeddings.shape[1]
    bucket = 2 * rows // wide_size
    values = embeddings.astype(jnp.float32)
    unit = (values * lax.rsqrt(jnp.sum(values * values, axis=1, keepdims=True) + 1e-06)).astype(
        jnp.bfloat16
    )
    owner = cluster_id // CPO
    owner_hot = (owner[:, None] == jnp.arange(wide_size, dtype=jnp.int32)[None, :]).astype(
        jnp.int32
    )
    earlier = jnp.cumsum(owner_hot, axis=0) - owner_hot
    slot = jnp.sum(earlier * owner_hot, axis=1)
    target = owner * bucket + slot
    send_rows = jnp.zeros((wide_size * bucket, width), jnp.bfloat16).at[target].set(unit)
    meta_rows = jnp.stack([cluster_id, order_index], axis=1)
    send_meta = jnp.full((wide_size * bucket, 2), -1, jnp.int32).at[target].set(meta_rows)
    held, held_meta = (
        lax.all_to_all(send_rows, "wide", split_axis=0, concat_axis=0, tiled=True),
        lax.all_to_all(send_meta, "wide", split_axis=0, concat_axis=0, tiled=True),
    )
    held_cl = held_meta[:, 0]
    held_or = held_meta[:, 1]
    live = held_cl >= 0
    start_best = jnp.full((held.shape[0],), -1.0, jnp.float32)

    def row_best(inner, other_cl, other_or):
        allowed = (
            (other_cl[None, :] == held_cl[:, None])
            & (other_or[None, :] < held_or[:, None])
            & live[:, None]
        )
        return jnp.max(jnp.where(allowed, inner, -1.0), axis=1)

    narrow_size = lax.axis_size("narrow")
    best = jnp.maximum(start_best, row_best(pair_inner(held, held), held_cl, held_or))
    for distance in range(1, narrow_size // 2 + 1):
        other_rows, other_meta = shifted((held, held_meta), "narrow", distance)
        other_cl = other_meta[:, 0]
        other_or = other_meta[:, 1]
        inner = pair_inner(held, other_rows)
        best = jnp.maximum(best, row_best(inner, other_cl, other_or))
        column_ok = (
            (held_cl[:, None] == other_cl[None, :])
            & (held_or[:, None] < other_or[None, :])
            & (other_cl[None, :] >= 0)
        )
        column_best = jnp.max(jnp.where(column_ok, inner, -1.0), axis=0)
        returned = shifted(column_best, "narrow", -distance)
        best = jnp.maximum(best, returned)
    answers = lax.all_to_all(best, "wide", split_axis=0, concat_axis=0, tiled=True)
    return answers[target]


CHUNKS = 4
MESH = pl.DeviceIdType.MESH


def meet_kernel(emb, meta, out, qraw, uq, kbuf, ku, qmeta, kmeta, racc, rres, cacc, cres,
                xs, xr, fs, fr, cs, cr, ms, mr, zs, zr, gs, zms, zmr, gms, rs, rr, ts, tr):
    w = lax.axis_index("wide")
    n = lax.axis_index("narrow")
    core = lax.rem(n, 2)
    near = n + 1 - 2 * core
    cross = lax.rem(n + 2, 4)
    far = lax.rem(near + 2, 4)
    peers = (near, cross, far)
    rows = emb.shape[0]
    piece = rows // CHUNKS

    def to_narrow(s, d, ss, rs_, who):
        return pltpu.make_async_remote_copy(s, d, ss, rs_, device_id={"narrow": who}, device_id_type=MESH)

    def to_wide(s, d, ss, rs_, who):
        return pltpu.make_async_remote_copy(s, d, ss, rs_, device_id={"wide": who}, device_id_type=MESH)

    barrier = pltpu.get_barrier_semaphore()
    for who in peers:
        pl.semaphore_signal(barrier, inc=1, device_id={"narrow": who}, device_id_type=MESH)
    for hop in range(1, 4):
        pl.semaphore_signal(barrier, inc=1, device_id={"wide": lax.rem(w + hop, 4)}, device_id_type=MESH)
    pl.semaphore_wait(barrier, 6)

    up = lax.rem(w + 1, 4)
    down = lax.rem(w + 3, 4)
    part = [pl.ds(c * piece, piece) for c in range(CHUNKS)]

    own_z = [to_wide(emb.at[part[c]], kbuf.at[0, part[c]], zs.at[c], zr.at[0, c], up) for c in range(CHUNKS)]
    own_zm = to_wide(meta, kmeta.at[0], zms, zmr.at[0], up)
    last_z = [to_wide(emb.at[part[c]], kbuf.at[2, part[c]], zs.at[c], zr.at[2, c], down) for c in range(CHUNKS)]
    last_zm = to_wide(meta, kmeta.at[2], zms, zmr.at[2], down)
    one_z = [to_wide(kbuf.at[0, part[c]], kbuf.at[1, part[c]], gs.at[0, c], zr.at[1, c], up) for c in range(CHUNKS)]
    one_zm = to_wide(kmeta.at[0], kmeta.at[1], gms.at[0], zmr.at[1], up)
    two_z = [to_wide(kbuf.at[0, part[c]], kbuf.at[0, part[c]], gs.at[0, c], zr.at[0, c], up) for c in range(CHUNKS)]
    two_zm = to_wide(kmeta.at[0], kmeta.at[0], gms.at[0], zmr.at[0], up)
    sec_z = [to_wide(kbuf.at[1, part[c]], kbuf.at[1, part[c]], gs.at[1, c], zr.at[1, c], up) for c in range(CHUNKS)]
    sec_zm = to_wide(kmeta.at[1], kmeta.at[1], gms.at[1], zmr.at[1], up)

    @pl.when(w < 2)
    def _():
        own_zm.start()
        for c in own_z:
            c.start()

    @pl.when(w == 3)
    def _():
        last_zm.start()
        for c in last_z:
            c.start()

    met = [to_narrow(meta, qmeta.at[j], ms.at[j], mr.at[j], peers[j]) for j in range(3)]
    xc = [to_narrow(emb.at[part[c]], qraw.at[1, part[c]], xs.at[c], xr.at[c], cross) for c in range(CHUNKS)]
    cc = to_narrow(emb, qraw.at[0], cs, cr, near)
    fc = [to_narrow(qraw.at[1, part[c]], qraw.at[2, part[c]], fs.at[c], fr.at[c], near) for c in range(CHUNKS)]
    for c in met:
        c.start()
    for c in xc:
        c.start()
    cc.start()

    def normed(ref):
        values = ref[...].astype(jnp.float32)
        return (values * lax.rsqrt(jnp.sum(values * values, axis=1, keepdims=True) + 1e-06)).astype(jnp.bfloat16)

    def tall(row):
        return jnp.broadcast_to(row, (rows, rows)).T

    def own_part(j, code, base, q_meta):
        inner = pair_inner(uq[0], uq[j])
        ok = (base == q_meta[1:2]) & (code < q_meta[0:1])
        racc[j] = jnp.max(jnp.where(ok, inner, -1.0), axis=0, keepdims=True)

    def met_by(slot):
        ku[...] = normed(kbuf.at[slot])
        code = tall(kmeta[slot][0:1])
        base = tall(kmeta[slot][1:2])
        col = jnp.full((rows, rows), -1.0, jnp.float32)
        for j in range(4):
            q_meta = meta[...] if j == 0 else qmeta[j - 1]
            inner = pair_inner(ku[...], uq[j])
            same = jnp.where(base == q_meta[1:2], inner, -1.0)
            before = code < q_meta[0:1]
            racc[j] = jnp.maximum(racc[j], jnp.max(jnp.where(before, same, -1.0), axis=0, keepdims=True))
            col = jnp.maximum(col, jnp.where(before, -1.0, same))
        cacc[slot] = jnp.max(col.T, axis=0, keepdims=True)

    uq[0] = normed(emb)
    own_code = tall(meta[0:1])
    own_base = tall(meta[1:2])
    own_part(0, own_code, own_base, meta[...])
    for c in met:
        c.wait_recv()
    cc.wait_recv()
    uq[1] = normed(qraw.at[0])
    own_part(1, own_code, own_base, qmeta[0])

    @pl.when(w >= 1)
    def _():
        own_zm.wait_recv()

    @pl.when(w == 1)
    def _():
        one_zm.start()

    @pl.when(w == 2)
    def _():
        two_zm.start()

    for c in range(CHUNKS):
        @pl.when(w >= 1)
        def _():
            own_z[c].wait_recv()

        @pl.when(w == 1)
        def _():
            one_z[c].start()

        @pl.when(w == 2)
        def _():
            two_z[c].start()

        xc[c].wait_recv()
        fc[c].start()

    uq[2] = normed(qraw.at[1])
    own_part(2, own_code, own_base, qmeta[1])
    for c in fc:
        c.wait_recv()
    uq[3] = normed(qraw.at[2])
    own_part(3, own_code, own_base, qmeta[2])

    back = [to_wide(cacc.at[s], cres.at[t], ts.at[s], tr.at[t], who)
            for s, t, who in ((0, 0, 0), (0, 1, 1), (0, 2, 1), (1, 1, 0), (1, 2, 0), (2, 1, 3))]

    @pl.when(w >= 1)
    def _():
        met_by(0)

    @pl.when(w == 1)
    def _():
        back[0].start()

    @pl.when(w == 2)
    def _():
        back[1].start()
        last_zm.wait_recv()
        for c in last_z:
            c.wait_recv()
        one_zm.wait_recv()
        sec_zm.start()
        for c in range(2):
            one_z[c].wait_recv()
            sec_z[c].start()
        met_by(2)
        back[5].start()
        for c in range(2, CHUNKS):
            one_z[c].wait_recv()
            sec_z[c].start()
        met_by(1)
        back[3].start()

    @pl.when(w == 3)
    def _():
        back[2].start()
        sec_zm.wait_recv()
        for c in sec_z:
            c.wait_recv()
        met_by(1)
        back[4].start()

    rowb = [to_narrow(racc.at[j + 1], rres.at[j], rs.at[j], rr.at[j], peers[j]) for j in range(3)]
    for c in rowb:
        c.start()
    for c in rowb:
        c.wait_recv()
    out[...] = jnp.maximum(jnp.maximum(racc[0], rres[0]), jnp.maximum(rres[1], rres[2]))

    @pl.when(w == 0)
    def _():
        for t in range(3):
            back[(0, 3, 4)[t]].wait_recv()
        out[...] = jnp.maximum(jnp.maximum(out[...], cres[0]), jnp.maximum(cres[1], cres[2]))
        own_zm.wait_send()
        for c in own_z:
            c.wait_send()

    @pl.when(w == 1)
    def _():
        back[1].wait_recv()
        back[2].wait_recv()
        out[...] = jnp.maximum(out[...], jnp.maximum(cres[1], cres[2]))
        own_zm.wait_send()
        one_zm.wait_send()
        for c in own_z + one_z:
            c.wait_send()
        back[0].wait_send()

    @pl.when(w == 2)
    def _():
        two_zm.wait_send()
        sec_zm.wait_send()
        for c in two_z + sec_z:
            c.wait_send()
        for i in (1, 5, 3):
            back[i].wait_send()

    @pl.when(w == 3)
    def _():
        back[5].wait_recv()
        out[...] = jnp.maximum(out[...], cres[1])
        last_zm.wait_send()
        for c in last_z:
            c.wait_send()
        back[2].wait_send()
        back[4].wait_send()

    for c in met + xc + [cc] + fc + rowb:
        c.wait_send()


def per_device_meet(embeddings, cluster_id, order_index):
    rows, width = embeddings.shape
    total = rows * lax.axis_size("wide") * lax.axis_size("narrow")
    base = cluster_id * total
    meta = jnp.stack([base + order_index, base]).astype(jnp.float32)
    dma = pltpu.SemaphoreType.DMA
    vmem = pl.BlockSpec(memory_space=pltpu.VMEM)
    wide_f = lambda k: pltpu.VMEM((k, 1, rows), jnp.float32)
    block = lambda k: pltpu.VMEM((k, rows, width), jnp.bfloat16)
    found = pl.pallas_call(
        meet_kernel,
        out_shape=jax.ShapeDtypeStruct((1, rows), jnp.float32),
        in_specs=[vmem, vmem],
        out_specs=vmem,
        scratch_shapes=[
            block(3), block(4), block(3), pltpu.VMEM((rows, width), jnp.bfloat16),
            pltpu.VMEM((3, 2, rows), jnp.float32), pltpu.VMEM((3, 2, rows), jnp.float32),
            wide_f(4), wide_f(3), wide_f(3), wide_f(3),
            dma((CHUNKS,)), dma((CHUNKS,)), dma((CHUNKS,)), dma((CHUNKS,)), dma, dma, dma((3,)), dma((3,)),
            dma((CHUNKS,)), dma((3, CHUNKS)), dma((2, CHUNKS)), dma, dma((3,)), dma((2,)),
            dma((3,)), dma((3,)), dma((3,)), dma((3,)),
        ],
        compiler_params=pltpu.CompilerParams(collective_id=0, has_side_effects=True),
    )(embeddings, meta)
    return found.reshape(rows)


def solution(mesh):
    meet = mesh.shape["wide"] == 4 and mesh.shape["narrow"] == 4
    return jax.shard_map(
        per_device_meet if meet else per_device,
        mesh=mesh,
        in_specs=(
            P(("parts", "wide", "narrow"), None),
            P(("parts", "wide", "narrow")),
            P(("parts", "wide", "narrow")),
        ),
        out_specs=P(("parts", "wide", "narrow")),
        check_vma=False,
    )
```

```python
import jax
import jax.numpy as jnp
from jax import lax
from jax.experimental import pallas as pl
from jax.experimental.pallas import tpu as pltpu
from jax.sharding import PartitionSpec as P

CPO = 16


def shifted(shard, axis, by):
    count = lax.axis_size(axis)
    return lax.ppermute(shard, axis, [(i, (i + by) % count) for i in range(count)])


def pair_inner(left, right):
    return lax.dot_general(
        left, right, (((1,), (1,)), ((), ())), preferred_element_type=jnp.float32
    )


def per_device(embeddings, cluster_id, order_index):
    wide_size = lax.axis_size("wide")
    rows = embeddings.shape[0]
    width = embeddings.shape[1]
    bucket = 2 * rows // wide_size
    values = embeddings.astype(jnp.float32)
    unit = (values * lax.rsqrt(jnp.sum(values * values, axis=1, keepdims=True) + 1e-06)).astype(
        jnp.bfloat16
    )
    owner = cluster_id // CPO
    owner_hot = (owner[:, None] == jnp.arange(wide_size, dtype=jnp.int32)[None, :]).astype(
        jnp.int32
    )
    earlier = jnp.cumsum(owner_hot, axis=0) - owner_hot
    slot = jnp.sum(earlier * owner_hot, axis=1)
    target = owner * bucket + slot
    send_rows = jnp.zeros((wide_size * bucket, width), jnp.bfloat16).at[target].set(unit)
    meta_rows = jnp.stack([cluster_id, order_index], axis=1)
    send_meta = jnp.full((wide_size * bucket, 2), -1, jnp.int32).at[target].set(meta_rows)
    held, held_meta = (
        lax.all_to_all(send_rows, "wide", split_axis=0, concat_axis=0, tiled=True),
        lax.all_to_all(send_meta, "wide", split_axis=0, concat_axis=0, tiled=True),
    )
    held_cl = held_meta[:, 0]
    held_or = held_meta[:, 1]
    live = held_cl >= 0
    start_best = jnp.full((held.shape[0],), -1.0, jnp.float32)

    def row_best(inner, other_cl, other_or):
        allowed = (
            (other_cl[None, :] == held_cl[:, None])
            & (other_or[None, :] < held_or[:, None])
            & live[:, None]
        )
        return jnp.max(jnp.where(allowed, inner, -1.0), axis=1)

    narrow_size = lax.axis_size("narrow")
    best = jnp.maximum(start_best, row_best(pair_inner(held, held), held_cl, held_or))
    for distance in range(1, narrow_size // 2 + 1):
        other_rows, other_meta = shifted((held, held_meta), "narrow", distance)
        other_cl = other_meta[:, 0]
        other_or = other_meta[:, 1]
        inner = pair_inner(held, other_rows)
        best = jnp.maximum(best, row_best(inner, other_cl, other_or))
        column_ok = (
            (held_cl[:, None] == other_cl[None, :])
            & (held_or[:, None] < other_or[None, :])
            & (other_cl[None, :] >= 0)
        )
        column_best = jnp.max(jnp.where(column_ok, inner, -1.0), axis=0)
        returned = shifted(column_best, "narrow", -distance)
        best = jnp.maximum(best, returned)
    answers = lax.all_to_all(best, "wide", split_axis=0, concat_axis=0, tiled=True)
    return answers[target]


CHUNKS = 4
SIDE = 4
MESH = pl.DeviceIdType.MESH


def meet_kernel(emb, cl, od, out, qraw, uq, acl, qod, pk, pm, kbuf, kmeta, target, racc, rres, cacc, cres, cfull,
                xs, xr, fs, fr, cs, cr, als, alr, ods, odr, zs, zr, zms, zmr, rs, rr, ts, tr):
    w = lax.axis_index("wide")
    n = lax.axis_index("narrow")
    near = n + 1 - 2 * lax.rem(n, 2)
    cross = lax.rem(n + 2, SIDE)
    far = lax.rem(near + 2, SIDE)
    peers = (near, cross, far)
    mate = w + 1 - 2 * lax.rem(w, 2)
    over = SIDE - 1 - w
    over_mate = over + 1 - 2 * lax.rem(over, 2)
    outer = (w == 0) | (w == SIDE - 1)
    inner = (w > 0) & (w < SIDE - 1)
    rows = emb.shape[0]
    half = rows // 2
    f32 = jnp.float32

    def send(s, d, ss, rs_, **who):
        return pltpu.make_async_remote_copy(s, d, ss, rs_, device_id=who, device_id_type=MESH)

    others = [(a, b) for a in range(SIDE) for b in range(SIDE) if a or b]
    barrier = pltpu.get_barrier_semaphore()
    for a, b in others:
        pl.semaphore_signal(
            barrier, inc=1, device_id={"wide": lax.rem(w + a, SIDE), "narrow": lax.rem(n + b, SIDE)}, device_id_type=MESH
        )
    pl.semaphore_wait(barrier, len(others))

    x_part = [pl.ds(c * (rows // CHUNKS), rows // CHUNKS) for c in range(CHUNKS)]
    z_part = [pl.ds(c * (half // CHUNKS), half // CHUNKS) for c in range(CHUNKS)]

    ids = [
        send(cl, acl.at[a * SIDE + b], als.at[a * SIDE + b], alr.at[a * SIDE + b],
             wide=lax.rem(w + a, SIDE), narrow=lax.rem(n + b, SIDE))
        for a, b in others
    ]
    orders = [send(od, qod.at[b - 1], ods.at[b - 1], odr.at[b - 1], narrow=lax.rem(n + b, SIDE)) for b in range(1, SIDE)]
    xc = [send(emb.at[p], qraw.at[1, p], xs.at[c], xr.at[c], narrow=cross) for c, p in enumerate(x_part)]
    cc = send(emb, qraw.at[0], cs, cr, narrow=near)
    fc = [send(qraw.at[1, p], qraw.at[2, p], fs.at[c], fr.at[c], narrow=near) for c, p in enumerate(x_part)]
    for c in ids[::-1] + orders + [cc] + xc:
        c.start()

    def normed(ref):
        values = ref[...].astype(f32)
        return (values * lax.rsqrt(jnp.sum(values * values, axis=1, keepdims=True) + 1e-06)).astype(jnp.bfloat16)

    def tall(row, across):
        return jnp.broadcast_to(row, (across, row.shape[1])).T

    def asked(j):
        if j == 0:
            return cl[...].astype(f32), od[...].astype(f32)
        if j == 2:
            return acl[2].astype(f32), qod[1].astype(f32)
        even = lax.rem(n, 2) == 0
        low, high = (3, 1) if j == 1 else (1, 3)
        slot = jnp.where(even, low, high)
        return acl[slot].astype(f32), qod[slot - 1].astype(f32)

    uq[0] = normed(emb)
    own_cl = tall(cl[...].astype(f32), rows)
    own_od = tall(od[...].astype(f32), rows)

    def own_part(j):
        q_cl, q_od = asked(j)
        ok = (own_cl == q_cl) & (own_od < q_od)
        racc[j] = jnp.max(jnp.where(ok, pair_inner(uq[0], uq[j]), -1.0), axis=0, keepdims=True)

    own_part(0)
    acl[0] = cl[...]
    for c in ids + orders:
        c.wait_recv()

    all_cl = acl[...].astype(f32)
    full = jnp.zeros((1, 1), f32)
    for o in range(SIDE)[::-1]:
        mine = (all_cl >= o * CPO) & (all_cl < (o + 1) * CPO)
        count = jnp.sum(jnp.where(mine, 1.0, 0.0), axis=2, keepdims=True)
        good = jnp.min(jnp.where(count == half, 1.0, 0.0), axis=0)
        full = jnp.where(good > 0.5, jnp.float32(o), full)
    id_row = cl[...].astype(f32)
    od_row = od[...].astype(f32)
    heavy = jnp.where((id_row >= full * CPO) & (id_row < (full + 1.0) * CPO), 1.0, 0.0)
    away = jnp.where(w < SIDE // 2, heavy, 1.0 - heavy)
    deep = lax.broadcasted_iota(jnp.int32, (rows, rows), 0)
    long = lax.broadcasted_iota(jnp.int32, (rows, rows), 1)
    tri = jnp.where(deep < long, 1.0, 0.0).astype(jnp.bfloat16)
    rank = jnp.dot(jnp.broadcast_to(away, (16, rows)).astype(jnp.bfloat16), tri, preferred_element_type=f32)[0:1]
    lane = lax.broadcasted_iota(jnp.int32, (1, rows), 1).astype(f32)
    place = jnp.where(away > 0.5, rank, half + lane - rank)
    target[...] = place
    pick = jnp.where(deep.astype(f32) == place, 1.0, 0.0).astype(jnp.bfloat16)
    od_high = jnp.floor(od_row * (1.0 / 128))
    od_low = od_row - od_high * 128
    tags = [jnp.broadcast_to(r, (16, rows)).astype(jnp.bfloat16) for r in (id_row, od_high, od_low)]
    tagged = [pair_inner(t, pick)[0:1] for t in tags]
    moved = jnp.concatenate([tagged[0], tagged[1] * 128 + tagged[2]], axis=0)
    pm[0] = moved[:, :half]
    pm[1] = moved[:, half:]
    for s in range(2):
        pk[s] = jnp.dot(pick[s * half:(s + 1) * half], uq[0], preferred_element_type=f32).astype(jnp.bfloat16)

    def row_of(src, dst, ss, slot, who):
        return [send(src.at[p], kbuf.at[dst, p], zs.at[ss, c], zr.at[slot, c], wide=who) for c, p in enumerate(z_part)]

    out_away = row_of(pk.at[0], 2, 0, 2, mate)
    out_home = row_of(pk.at[1], 3, 1, 3, mate)
    in_away = row_of(pk.at[0], 0, 0, 0, over)
    in_next = row_of(kbuf.at[2], 1, 1, 1, over)
    on_near = row_of(kbuf.at[0], 0, 2, 0, mate)
    on_far = row_of(kbuf.at[1], 1, 3, 1, mate)

    def tag_of(src, dst, ss, who):
        return send(src, kmeta.at[dst], zms.at[ss], zmr.at[dst], wide=who)

    t_out_away = tag_of(pm.at[0], 2, 0, mate)
    t_out_home = tag_of(pm.at[1], 3, 1, mate)
    t_in_away = tag_of(pm.at[0], 0, 0, over)
    t_in_next = tag_of(kmeta.at[2], 1, 1, over)
    t_on_near = tag_of(kmeta.at[0], 0, 2, mate)
    t_on_far = tag_of(kmeta.at[1], 1, 3, mate)

    @pl.when(outer)
    def _():
        t_out_away.start()
        t_out_home.start()
        for c in out_away + out_home:
            c.start()

    @pl.when(inner)
    def _():
        t_in_away.start()
        for c in in_away:
            c.start()

    cc.wait_recv()
    uq[1] = normed(qraw.at[0])
    own_part(1)

    @pl.when(inner)
    def _():
        t_out_away.wait_recv()
        t_in_next.start()
        t_in_away.wait_recv()
        t_on_near.start()

    for c in range(CHUNKS):
        xc[c].wait_recv()
        fc[c].start()

        @pl.when(inner)
        def _():
            out_away[c].wait_recv()
            in_next[c].start()
            in_away[c].wait_recv()
            on_near[c].start()

    uq[2] = normed(qraw.at[1])
    own_part(2)

    @pl.when(inner)
    def _():
        t_in_next.wait_recv()
        t_on_far.start()
        in_next[0].wait_recv()
        on_far[0].start()

    for c in fc:
        c.wait_recv()
    uq[3] = normed(qraw.at[2])
    own_part(3)

    def met_by(slot):
        k_cl = tall(kmeta[slot][0:1], rows)
        k_od = tall(kmeta[slot][1:2], rows)
        col = jnp.full((half, rows), -1.0, f32)
        for j in range(4):
            q_cl, q_od = asked(j)
            same = jnp.where(k_cl == q_cl, pair_inner(kbuf[slot], uq[j]), -1.0)
            before = k_od < q_od
            racc[j] = jnp.maximum(racc[j], jnp.max(jnp.where(before, same, -1.0), axis=0, keepdims=True))
            col = jnp.maximum(col, jnp.where(before, -1.0, same))
        cacc[slot] = jnp.max(col.T, axis=0, keepdims=True)

    def back(slot, dst, who):
        return send(cacc.at[slot], cres.at[dst], ts.at[slot], tr.at[dst], wide=who)

    b_in = [back(0, 0, over), back(1, 0, over_mate), back(2, 2, mate), back(3, 3, mate)]
    b_out = [back(0, 1, over_mate), back(1, 1, over)]

    @pl.when(inner)
    def _():
        in_next[1].wait_recv()
        on_far[1].start()
        met_by(0)
        b_in[0].start()
        for c in range(2, CHUNKS):
            in_next[c].wait_recv()
            on_far[c].start()
        met_by(1)
        b_in[1].start()
        t_out_home.wait_recv()
        for c in out_home:
            c.wait_recv()
        met_by(2)
        b_in[2].start()
        met_by(3)
        b_in[3].start()

    @pl.when(outer)
    def _():
        t_on_near.wait_recv()
        for c in on_near:
            c.wait_recv()
        met_by(0)
        b_out[0].start()
        t_on_far.wait_recv()
        for c in on_far:
            c.wait_recv()
        met_by(1)
        b_out[1].start()

    rowb = [send(racc.at[j + 1], rres.at[j], rs.at[j], rr.at[j], narrow=peers[j]) for j in range(3)]
    for c in rowb:
        c.start()
    for c in rowb:
        c.wait_recv()
    b_in[0].wait_recv()
    b_out[0].wait_recv()
    cfull[:, :half] = jnp.maximum(cres[0], cres[1])
    cfull[:, half:] = jnp.full((1, half), -1.0, f32)

    @pl.when(outer)
    def _():
        b_in[2].wait_recv()
        b_in[3].wait_recv()
        cfull[:, :half] = jnp.maximum(cfull[:, :half], cres[2])
        cfull[:, half:] = cres[3]

    mine = jnp.where(deep.astype(f32) == target[...], tall(cfull[...], rows), -1.0)
    best = jnp.maximum(jnp.maximum(racc[0], rres[0]), jnp.maximum(rres[1], rres[2]))
    out[...] = jnp.maximum(best, jnp.max(mine, axis=0, keepdims=True))

    @pl.when(outer)
    def _():
        for c in [t_out_away, t_out_home] + out_away + out_home + b_out:
            c.wait_send()

    @pl.when(inner)
    def _():
        for c in [t_in_away, t_in_next, t_on_near, t_on_far] + in_away + in_next + on_near + on_far + b_in:
            c.wait_send()

    for c in ids + orders + xc + [cc] + fc + rowb:
        c.wait_send()


def per_device_meet(embeddings, cluster_id, order_index):
    rows, width = embeddings.shape
    half = rows // 2
    dma = pltpu.SemaphoreType.DMA
    vmem = pl.BlockSpec(memory_space=pltpu.VMEM)
    line = lambda k, m: pltpu.VMEM((k, 1, m), jnp.float32)
    block = lambda k, m: pltpu.VMEM((k, m, width), jnp.bfloat16)
    found = pl.pallas_call(
        meet_kernel,
        out_shape=jax.ShapeDtypeStruct((1, rows), jnp.float32),
        in_specs=[vmem, vmem, vmem],
        out_specs=vmem,
        scratch_shapes=[
            block(3, rows), block(4, rows),
            pltpu.VMEM((SIDE * SIDE, 1, rows), jnp.int32), pltpu.VMEM((3, 1, rows), jnp.int32),
            block(2, half), pltpu.VMEM((2, 2, half), jnp.float32),
            block(4, half), pltpu.VMEM((4, 2, half), jnp.float32),
            pltpu.VMEM((1, rows), jnp.float32),
            line(4, rows), line(3, rows), line(4, half), line(4, half), pltpu.VMEM((1, rows), jnp.float32),
            dma((CHUNKS,)), dma((CHUNKS,)), dma((CHUNKS,)), dma((CHUNKS,)), dma, dma,
            dma((SIDE * SIDE,)), dma((SIDE * SIDE,)), dma((3,)), dma((3,)),
            dma((4, CHUNKS)), dma((4, CHUNKS)), dma((4,)), dma((4,)),
            dma((3,)), dma((3,)), dma((4,)), dma((4,)),
        ],
        compiler_params=pltpu.CompilerParams(collective_id=0, has_side_effects=True),
    )(embeddings, cluster_id.reshape(1, rows), order_index.reshape(1, rows))
    return jnp.maximum(found.reshape(rows), -1.0)


def solution(mesh):
    meet = mesh.shape["wide"] == SIDE and mesh.shape["narrow"] == SIDE
    return jax.shard_map(
        per_device_meet if meet else per_device,
        mesh=mesh,
        in_specs=(
            P(("parts", "wide", "narrow"), None),
            P(("parts", "wide", "narrow")),
            P(("parts", "wide", "narrow")),
        ),
        out_specs=P(("parts", "wide", "narrow")),
        check_vma=False,
    )
```

```python
import jax
import jax.numpy as jnp
from jax import lax
from jax.experimental import pallas as pl
from jax.experimental.pallas import tpu as pltpu
from jax.sharding import PartitionSpec as P

CPO = 16


def shifted(shard, axis, by):
    count = lax.axis_size(axis)
    return lax.ppermute(shard, axis, [(i, (i + by) % count) for i in range(count)])


def pair_inner(left, right):
    return lax.dot_general(
        left, right, (((1,), (1,)), ((), ())), preferred_element_type=jnp.float32
    )


def per_device(embeddings, cluster_id, order_index):
    wide_size = lax.axis_size("wide")
    rows = embeddings.shape[0]
    width = embeddings.shape[1]
    bucket = 2 * rows // wide_size
    values = embeddings.astype(jnp.float32)
    unit = (values * lax.rsqrt(jnp.sum(values * values, axis=1, keepdims=True) + 1e-06)).astype(
        jnp.bfloat16
    )
    owner = cluster_id // CPO
    owner_hot = (owner[:, None] == jnp.arange(wide_size, dtype=jnp.int32)[None, :]).astype(
        jnp.int32
    )
    earlier = jnp.cumsum(owner_hot, axis=0) - owner_hot
    slot = jnp.sum(earlier * owner_hot, axis=1)
    target = owner * bucket + slot
    send_rows = jnp.zeros((wide_size * bucket, width), jnp.bfloat16).at[target].set(unit)
    meta_rows = jnp.stack([cluster_id, order_index], axis=1)
    send_meta = jnp.full((wide_size * bucket, 2), -1, jnp.int32).at[target].set(meta_rows)
    held, held_meta = (
        lax.all_to_all(send_rows, "wide", split_axis=0, concat_axis=0, tiled=True),
        lax.all_to_all(send_meta, "wide", split_axis=0, concat_axis=0, tiled=True),
    )
    held_cl = held_meta[:, 0]
    held_or = held_meta[:, 1]
    live = held_cl >= 0
    start_best = jnp.full((held.shape[0],), -1.0, jnp.float32)

    def row_best(inner, other_cl, other_or):
        allowed = (
            (other_cl[None, :] == held_cl[:, None])
            & (other_or[None, :] < held_or[:, None])
            & live[:, None]
        )
        return jnp.max(jnp.where(allowed, inner, -1.0), axis=1)

    narrow_size = lax.axis_size("narrow")
    best = jnp.maximum(start_best, row_best(pair_inner(held, held), held_cl, held_or))
    for distance in range(1, narrow_size // 2 + 1):
        other_rows, other_meta = shifted((held, held_meta), "narrow", distance)
        other_cl = other_meta[:, 0]
        other_or = other_meta[:, 1]
        inner = pair_inner(held, other_rows)
        best = jnp.maximum(best, row_best(inner, other_cl, other_or))
        column_ok = (
            (held_cl[:, None] == other_cl[None, :])
            & (held_or[:, None] < other_or[None, :])
            & (other_cl[None, :] >= 0)
        )
        column_best = jnp.max(jnp.where(column_ok, inner, -1.0), axis=0)
        returned = shifted(column_best, "narrow", -distance)
        best = jnp.maximum(best, returned)
    answers = lax.all_to_all(best, "wide", split_axis=0, concat_axis=0, tiled=True)
    return answers[target]


CHUNKS = 4
SIDE = 4
MESH = pl.DeviceIdType.MESH


def meet_kernel(emb_far, cl, od, out, emb, got, qraw, uq, acl, qod, pk, pm, kbuf, kmeta, target, racc, rres, cacc, cres, cfull,
                xs, xr, fs, fr, cs, cr, als, alr, ods, odr, zs, zr, zms, zmr, rs, rr, ts, tr):
    w = lax.axis_index("wide")
    n = lax.axis_index("narrow")
    near = n + 1 - 2 * lax.rem(n, 2)
    cross = lax.rem(n + 2, SIDE)
    far = lax.rem(near + 2, SIDE)
    peers = (near, cross, far)
    mate = w + 1 - 2 * lax.rem(w, 2)
    over = SIDE - 1 - w
    over_mate = over + 1 - 2 * lax.rem(over, 2)
    outer = (w == 0) | (w == SIDE - 1)
    inner = (w > 0) & (w < SIDE - 1)
    rows = emb.shape[0]
    half = rows // 2
    f32 = jnp.float32

    def send(s, d, ss, rs_, **who):
        return pltpu.make_async_remote_copy(s, d, ss, rs_, device_id=who, device_id_type=MESH)

    others = [(a, b) for a in range(SIDE) for b in range(SIDE) if a or b]
    barrier = pltpu.get_barrier_semaphore()
    for a, b in others:
        pl.semaphore_signal(
            barrier, inc=1, device_id={"wide": lax.rem(w + a, SIDE), "narrow": lax.rem(n + b, SIDE)}, device_id_type=MESH
        )
    take = pltpu.make_async_copy(emb_far, emb, got)
    take.start()
    pl.semaphore_wait(barrier, len(others))

    x_part = [pl.ds(c * (rows // CHUNKS), rows // CHUNKS) for c in range(CHUNKS)]
    z_part = [pl.ds(c * (half // CHUNKS), half // CHUNKS) for c in range(CHUNKS)]

    ids = [
        send(cl, acl.at[a * SIDE + b], als.at[a * SIDE + b], alr.at[a * SIDE + b],
             wide=lax.rem(w + a, SIDE), narrow=lax.rem(n + b, SIDE))
        for a, b in others
    ]
    orders = [send(od, qod.at[b - 1], ods.at[b - 1], odr.at[b - 1], narrow=lax.rem(n + b, SIDE)) for b in range(1, SIDE)]
    xc = [send(emb.at[p], qraw.at[1, p], xs.at[c], xr.at[c], narrow=cross) for c, p in enumerate(x_part)]
    cc = send(emb, qraw.at[0], cs, cr, narrow=near)
    fc = [send(qraw.at[1, p], qraw.at[2, p], fs.at[c], fr.at[c], narrow=near) for c, p in enumerate(x_part)]
    for c in ids[::-1] + orders:
        c.start()
    take.wait()
    for c in xc + [cc]:
        c.start()

    def normed(ref):
        values = ref[...].astype(f32)
        return (values * lax.rsqrt(jnp.sum(values * values, axis=1, keepdims=True) + 1e-06)).astype(jnp.bfloat16)

    def tall(row, across):
        return jnp.broadcast_to(row, (across, row.shape[1])).T

    def asked(j):
        if j == 0:
            return cl[...].astype(f32), od[...].astype(f32)
        if j == 2:
            return acl[2].astype(f32), qod[1].astype(f32)
        even = lax.rem(n, 2) == 0
        low, high = (3, 1) if j == 1 else (1, 3)
        slot = jnp.where(even, low, high)
        return acl[slot].astype(f32), qod[slot - 1].astype(f32)

    uq[0] = normed(emb)
    own_cl = tall(cl[...].astype(f32), rows)
    own_od = tall(od[...].astype(f32), rows)

    def own_part(j):
        q_cl, q_od = asked(j)
        ok = (own_cl == q_cl) & (own_od < q_od)
        racc[j] = jnp.max(jnp.where(ok, pair_inner(uq[0], uq[j]), -1.0), axis=0, keepdims=True)

    own_part(0)
    acl[0] = cl[...]
    for c in ids + orders:
        c.wait_recv()

    all_cl = acl[...].astype(f32)
    full = jnp.zeros((1, 1), f32)
    for o in range(SIDE)[::-1]:
        mine = (all_cl >= o * CPO) & (all_cl < (o + 1) * CPO)
        count = jnp.sum(jnp.where(mine, 1.0, 0.0), axis=2, keepdims=True)
        good = jnp.min(jnp.where(count == half, 1.0, 0.0), axis=0)
        full = jnp.where(good > 0.5, jnp.float32(o), full)
    id_row = cl[...].astype(f32)
    od_row = od[...].astype(f32)
    heavy = jnp.where((id_row >= full * CPO) & (id_row < (full + 1.0) * CPO), 1.0, 0.0)
    away = jnp.where(w < SIDE // 2, heavy, 1.0 - heavy)
    deep = lax.broadcasted_iota(jnp.int32, (rows, rows), 0)
    long = lax.broadcasted_iota(jnp.int32, (rows, rows), 1)
    tri = jnp.where(deep < long, 1.0, 0.0).astype(jnp.bfloat16)
    rank = jnp.dot(jnp.broadcast_to(away, (16, rows)).astype(jnp.bfloat16), tri, preferred_element_type=f32)[0:1]
    lane = lax.broadcasted_iota(jnp.int32, (1, rows), 1).astype(f32)
    place = jnp.where(away > 0.5, rank, half + lane - rank)
    target[...] = place
    pick = jnp.where(deep.astype(f32) == place, 1.0, 0.0).astype(jnp.bfloat16)
    od_high = jnp.floor(od_row * (1.0 / 128))
    od_low = od_row - od_high * 128
    tags = [jnp.broadcast_to(r, (16, rows)).astype(jnp.bfloat16) for r in (id_row, od_high, od_low)]
    tagged = [pair_inner(t, pick)[0:1] for t in tags]
    moved = jnp.concatenate([tagged[0], tagged[1] * 128 + tagged[2]], axis=0)
    pm[0] = moved[:, :half]
    pm[1] = moved[:, half:]
    for s in range(2):
        pk[s] = jnp.dot(pick[s * half:(s + 1) * half], uq[0], preferred_element_type=f32).astype(jnp.bfloat16)

    def row_of(src, dst, ss, slot, who):
        return [send(src.at[p], kbuf.at[dst, p], zs.at[ss, c], zr.at[slot, c], wide=who) for c, p in enumerate(z_part)]

    out_away = row_of(pk.at[0], 2, 0, 2, mate)
    out_home = row_of(pk.at[1], 3, 1, 3, mate)
    in_away = row_of(pk.at[0], 0, 0, 0, over)
    in_next = row_of(kbuf.at[2], 1, 1, 1, over)
    on_near = row_of(kbuf.at[0], 0, 2, 0, mate)
    on_far = row_of(kbuf.at[1], 1, 3, 1, mate)

    def tag_of(src, dst, ss, who):
        return send(src, kmeta.at[dst], zms.at[ss], zmr.at[dst], wide=who)

    t_out_away = tag_of(pm.at[0], 2, 0, mate)
    t_out_home = tag_of(pm.at[1], 3, 1, mate)
    t_in_away = tag_of(pm.at[0], 0, 0, over)
    t_in_next = tag_of(kmeta.at[2], 1, 1, over)
    t_on_near = tag_of(kmeta.at[0], 0, 2, mate)
    t_on_far = tag_of(kmeta.at[1], 1, 3, mate)

    @pl.when(outer)
    def _():
        t_out_away.start()
        t_out_home.start()
        for c in out_away + out_home:
            c.start()

    @pl.when(inner)
    def _():
        t_in_away.start()
        for c in in_away:
            c.start()

    cc.wait_recv()
    uq[1] = normed(qraw.at[0])
    own_part(1)

    @pl.when(inner)
    def _():
        t_out_away.wait_recv()
        t_in_next.start()
        t_in_away.wait_recv()
        t_on_near.start()

    for c in range(CHUNKS):
        xc[c].wait_recv()
        fc[c].start()

        @pl.when(inner)
        def _():
            out_away[c].wait_recv()
            in_next[c].start()
            in_away[c].wait_recv()
            on_near[c].start()

    uq[2] = normed(qraw.at[1])
    own_part(2)

    @pl.when(inner)
    def _():
        t_in_next.wait_recv()
        t_on_far.start()
        in_next[0].wait_recv()
        on_far[0].start()

    for c in fc:
        c.wait_recv()
    uq[3] = normed(qraw.at[2])
    own_part(3)

    def met_by(slot):
        k_cl = tall(kmeta[slot][0:1], rows)
        k_od = tall(kmeta[slot][1:2], rows)
        col = jnp.full((half, rows), -1.0, f32)
        for j in range(4):
            q_cl, q_od = asked(j)
            same = jnp.where(k_cl == q_cl, pair_inner(kbuf[slot], uq[j]), -1.0)
            before = k_od < q_od
            racc[j] = jnp.maximum(racc[j], jnp.max(jnp.where(before, same, -1.0), axis=0, keepdims=True))
            col = jnp.maximum(col, jnp.where(before, -1.0, same))
        cacc[slot] = jnp.max(col.T, axis=0, keepdims=True)

    def back(slot, dst, who):
        return send(cacc.at[slot], cres.at[dst], ts.at[slot], tr.at[dst], wide=who)

    b_in = [back(0, 0, over), back(1, 0, over_mate), back(2, 2, mate), back(3, 3, mate)]
    b_out = [back(0, 1, over_mate), back(1, 1, over)]

    @pl.when(inner)
    def _():
        in_next[1].wait_recv()
        on_far[1].start()
        met_by(0)
        b_in[0].start()
        for c in range(2, CHUNKS):
            in_next[c].wait_recv()
            on_far[c].start()
        met_by(1)
        b_in[1].start()
        t_out_home.wait_recv()
        for c in out_home:
            c.wait_recv()
        met_by(2)
        b_in[2].start()
        met_by(3)
        b_in[3].start()

    @pl.when(outer)
    def _():
        t_on_near.wait_recv()
        for c in on_near:
            c.wait_recv()
        met_by(0)
        b_out[0].start()
        t_on_far.wait_recv()
        for c in on_far:
            c.wait_recv()
        met_by(1)
        b_out[1].start()

    rowb = [send(racc.at[j + 1], rres.at[j], rs.at[j], rr.at[j], narrow=peers[j]) for j in range(3)]
    for c in rowb:
        c.start()
    for c in rowb:
        c.wait_recv()
    b_in[0].wait_recv()
    b_out[0].wait_recv()
    cfull[:, :half] = jnp.maximum(cres[0], cres[1])
    cfull[:, half:] = jnp.full((1, half), -1.0, f32)

    @pl.when(outer)
    def _():
        b_in[2].wait_recv()
        b_in[3].wait_recv()
        cfull[:, :half] = jnp.maximum(cfull[:, :half], cres[2])
        cfull[:, half:] = cres[3]

    mine = jnp.where(deep.astype(f32) == target[...], tall(cfull[...], rows), -1.0)
    best = jnp.maximum(jnp.maximum(racc[0], rres[0]), jnp.maximum(rres[1], rres[2]))
    out[...] = jnp.maximum(best, jnp.max(mine, axis=0, keepdims=True))

    @pl.when(outer)
    def _():
        for c in [t_out_away, t_out_home] + out_away + out_home + b_out:
            c.wait_send()

    @pl.when(inner)
    def _():
        for c in [t_in_away, t_in_next, t_on_near, t_on_far] + in_away + in_next + on_near + on_far + b_in:
            c.wait_send()

    for c in ids + orders + xc + [cc] + fc + rowb:
        c.wait_send()


def per_device_meet(embeddings, cluster_id, order_index):
    rows, width = embeddings.shape
    half = rows // 2
    dma = pltpu.SemaphoreType.DMA
    vmem = pl.BlockSpec(memory_space=pltpu.VMEM)
    line = lambda k, m: pltpu.VMEM((k, 1, m), jnp.float32)
    block = lambda k, m: pltpu.VMEM((k, m, width), jnp.bfloat16)
    found = pl.pallas_call(
        meet_kernel,
        out_shape=jax.ShapeDtypeStruct((1, rows), jnp.float32),
        in_specs=[pl.BlockSpec(memory_space=pl.ANY), vmem, vmem],
        out_specs=vmem,
        scratch_shapes=[
            pltpu.VMEM((rows, width), jnp.bfloat16), dma, block(3, rows), block(4, rows),
            pltpu.VMEM((SIDE * SIDE, 1, rows), jnp.int32), pltpu.VMEM((3, 1, rows), jnp.int32),
            block(2, half), pltpu.VMEM((2, 2, half), jnp.float32),
            block(4, half), pltpu.VMEM((4, 2, half), jnp.float32),
            pltpu.VMEM((1, rows), jnp.float32),
            line(4, rows), line(3, rows), line(4, half), line(4, half), pltpu.VMEM((1, rows), jnp.float32),
            dma((CHUNKS,)), dma((CHUNKS,)), dma((CHUNKS,)), dma((CHUNKS,)), dma, dma,
            dma((SIDE * SIDE,)), dma((SIDE * SIDE,)), dma((3,)), dma((3,)),
            dma((4, CHUNKS)), dma((4, CHUNKS)), dma((4,)), dma((4,)),
            dma((3,)), dma((3,)), dma((4,)), dma((4,)),
        ],
        compiler_params=pltpu.CompilerParams(collective_id=0, has_side_effects=True),
    )(embeddings, cluster_id.reshape(1, rows), order_index.reshape(1, rows))
    return jnp.maximum(found.reshape(rows), -1.0)


def solution(mesh):
    meet = mesh.shape["wide"] == SIDE and mesh.shape["narrow"] == SIDE
    return jax.shard_map(
        per_device_meet if meet else per_device,
        mesh=mesh,
        in_specs=(
            P(("parts", "wide", "narrow"), None),
            P(("parts", "wide", "narrow")),
            P(("parts", "wide", "narrow")),
        ),
        out_specs=P(("parts", "wide", "narrow")),
        check_vma=False,
    )
```

```python
import jax
import jax.numpy as jnp
from jax import lax
from jax.experimental import pallas as pl
from jax.experimental.pallas import tpu as pltpu
from jax.sharding import PartitionSpec as P

CPO = 16


def shifted(shard, axis, by):
    count = lax.axis_size(axis)
    return lax.ppermute(shard, axis, [(i, (i + by) % count) for i in range(count)])


def pair_inner(left, right):
    return lax.dot_general(
        left, right, (((1,), (1,)), ((), ())), preferred_element_type=jnp.float32
    )


def per_device(embeddings, cluster_id, order_index):
    wide_size = lax.axis_size("wide")
    rows = embeddings.shape[0]
    width = embeddings.shape[1]
    bucket = 2 * rows // wide_size
    values = embeddings.astype(jnp.float32)
    unit = (values * lax.rsqrt(jnp.sum(values * values, axis=1, keepdims=True) + 1e-06)).astype(
        jnp.bfloat16
    )
    owner = cluster_id // CPO
    owner_hot = (owner[:, None] == jnp.arange(wide_size, dtype=jnp.int32)[None, :]).astype(
        jnp.int32
    )
    earlier = jnp.cumsum(owner_hot, axis=0) - owner_hot
    slot = jnp.sum(earlier * owner_hot, axis=1)
    target = owner * bucket + slot
    send_rows = jnp.zeros((wide_size * bucket, width), jnp.bfloat16).at[target].set(unit)
    meta_rows = jnp.stack([cluster_id, order_index], axis=1)
    send_meta = jnp.full((wide_size * bucket, 2), -1, jnp.int32).at[target].set(meta_rows)
    held, held_meta = (
        lax.all_to_all(send_rows, "wide", split_axis=0, concat_axis=0, tiled=True),
        lax.all_to_all(send_meta, "wide", split_axis=0, concat_axis=0, tiled=True),
    )
    held_cl = held_meta[:, 0]
    held_or = held_meta[:, 1]
    live = held_cl >= 0
    start_best = jnp.full((held.shape[0],), -1.0, jnp.float32)

    def row_best(inner, other_cl, other_or):
        allowed = (
            (other_cl[None, :] == held_cl[:, None])
            & (other_or[None, :] < held_or[:, None])
            & live[:, None]
        )
        return jnp.max(jnp.where(allowed, inner, -1.0), axis=1)

    narrow_size = lax.axis_size("narrow")
    best = jnp.maximum(start_best, row_best(pair_inner(held, held), held_cl, held_or))
    for distance in range(1, narrow_size // 2 + 1):
        other_rows, other_meta = shifted((held, held_meta), "narrow", distance)
        other_cl = other_meta[:, 0]
        other_or = other_meta[:, 1]
        inner = pair_inner(held, other_rows)
        best = jnp.maximum(best, row_best(inner, other_cl, other_or))
        column_ok = (
            (held_cl[:, None] == other_cl[None, :])
            & (held_or[:, None] < other_or[None, :])
            & (other_cl[None, :] >= 0)
        )
        column_best = jnp.max(jnp.where(column_ok, inner, -1.0), axis=0)
        returned = shifted(column_best, "narrow", -distance)
        best = jnp.maximum(best, returned)
    answers = lax.all_to_all(best, "wide", split_axis=0, concat_axis=0, tiled=True)
    return answers[target]


CHUNKS = 4
SIDE = 4
MESH = pl.DeviceIdType.MESH


def meet_kernel(emb_far, cl, od, out, emb, got, qraw, uq, acl, qod, pk, pm, kbuf, kmeta, target, racc, rres, cacc, cres, cfull,
                xs, xr, fs, fr, cs, cr, als, alr, ods, odr, zs, zr, zms, zmr, rs, rr, ts, tr):
    w = lax.axis_index("wide")
    n = lax.axis_index("narrow")
    near = n + 1 - 2 * lax.rem(n, 2)
    cross = lax.rem(n + 2, SIDE)
    far = lax.rem(near + 2, SIDE)
    peers = (near, cross, far)
    mate = w + 1 - 2 * lax.rem(w, 2)
    over = SIDE - 1 - w
    over_mate = over + 1 - 2 * lax.rem(over, 2)
    outer = (w == 0) | (w == SIDE - 1)
    inner = (w > 0) & (w < SIDE - 1)
    rows = emb.shape[0]
    half = rows // 2
    f32 = jnp.float32

    def send(s, d, ss, rs_, **who):
        return pltpu.make_async_remote_copy(s, d, ss, rs_, device_id=who, device_id_type=MESH)

    others = [(a, b) for a in range(SIDE) for b in range(SIDE) if a or b]
    barrier = pltpu.get_barrier_semaphore()
    for a, b in others:
        pl.semaphore_signal(
            barrier, inc=1, device_id={"wide": lax.rem(w + a, SIDE), "narrow": lax.rem(n + b, SIDE)}, device_id_type=MESH
        )
    take = pltpu.make_async_copy(emb_far, emb, got)
    take.start()
    pl.semaphore_wait(barrier, len(others))

    x_part = [pl.ds(c * (rows // CHUNKS), rows // CHUNKS) for c in range(CHUNKS)]
    z_part = [pl.ds(c * (half // CHUNKS), half // CHUNKS) for c in range(CHUNKS)]

    ids = [
        send(cl, acl.at[a * SIDE + b], als.at[a * SIDE + b], alr.at[a * SIDE + b],
             wide=lax.rem(w + a, SIDE), narrow=lax.rem(n + b, SIDE))
        for a, b in others
    ]
    orders = [send(od, qod.at[b - 1], ods.at[b - 1], odr.at[b - 1], narrow=lax.rem(n + b, SIDE)) for b in range(1, SIDE)]
    xc = [send(emb.at[p], qraw.at[1, p], xs.at[c], xr.at[c], narrow=cross) for c, p in enumerate(x_part)]
    cc = send(emb, qraw.at[0], cs, cr, narrow=near)
    fc = [send(qraw.at[1, p], qraw.at[2, p], fs.at[c], fr.at[c], narrow=near) for c, p in enumerate(x_part)]
    for c in ids[::-1] + orders:
        c.start()
    take.wait()
    for c in xc + [cc]:
        c.start()

    def normed(ref):
        values = ref[...].astype(f32)
        return (values * lax.rsqrt(jnp.sum(values * values, axis=1, keepdims=True) + 1e-06)).astype(jnp.bfloat16)

    def tall(row, across):
        return jnp.broadcast_to(row, (across, row.shape[1])).T

    def asked(j):
        if j == 0:
            return cl[...].astype(f32), od[...].astype(f32)
        if j == 2:
            return acl[2].astype(f32), qod[1].astype(f32)
        even = lax.rem(n, 2) == 0
        low, high = (3, 1) if j == 1 else (1, 3)
        slot = jnp.where(even, low, high)
        return acl[slot].astype(f32), qod[slot - 1].astype(f32)

    uq[0] = normed(emb)
    own_cl = tall(cl[...].astype(f32), rows)
    own_od = tall(od[...].astype(f32), rows)

    def own_part(j):
        q_cl, q_od = asked(j)
        ok = (own_cl == q_cl) & (own_od < q_od)
        racc[j] = jnp.max(jnp.where(ok, pair_inner(uq[0], uq[j]), -1.0), axis=0, keepdims=True)

    own_part(0)
    acl[0] = cl[...]
    for c in ids + orders:
        c.wait_recv()

    all_cl = acl[...].astype(f32)
    full = jnp.zeros((1, 1), f32)
    for o in range(SIDE)[::-1]:
        mine = (all_cl >= o * CPO) & (all_cl < (o + 1) * CPO)
        count = jnp.sum(jnp.where(mine, 1.0, 0.0), axis=2, keepdims=True)
        good = jnp.min(jnp.where(count == half, 1.0, 0.0), axis=0)
        full = jnp.where(good > 0.5, jnp.float32(o), full)
    id_row = cl[...].astype(f32)
    od_row = od[...].astype(f32)
    heavy = jnp.where((id_row >= full * CPO) & (id_row < (full + 1.0) * CPO), 1.0, 0.0)
    away = jnp.where(w < SIDE // 2, heavy, 1.0 - heavy)
    deep = lax.broadcasted_iota(jnp.int32, (rows, rows), 0)
    long = lax.broadcasted_iota(jnp.int32, (rows, rows), 1)
    tri = jnp.where(deep < long, 1.0, 0.0).astype(jnp.bfloat16)
    rank = jnp.dot(jnp.broadcast_to(away, (16, rows)).astype(jnp.bfloat16), tri, preferred_element_type=f32)[0:1]
    lane = lax.broadcasted_iota(jnp.int32, (1, rows), 1).astype(f32)
    place = jnp.where(away > 0.5, rank, half + lane - rank)
    target[...] = place
    pick = jnp.where(deep.astype(f32) == place, 1.0, 0.0).astype(jnp.bfloat16)
    od_high = jnp.floor(od_row * (1.0 / 128))
    od_low = od_row - od_high * 128
    tags = [jnp.broadcast_to(r, (16, rows)).astype(jnp.bfloat16) for r in (id_row, od_high, od_low)]
    tagged = [pair_inner(t, pick)[0:1] for t in tags]
    moved = jnp.concatenate([tagged[0], tagged[1] * 128 + tagged[2]], axis=0)
    pm[0] = moved[:, :half]
    pm[1] = moved[:, half:]
    for s in range(2):
        pk[s] = jnp.dot(pick[s * half:(s + 1) * half], uq[0], preferred_element_type=f32).astype(jnp.bfloat16)

    def row_of(src, dst, ss, slot, who):
        return [send(src.at[p], kbuf.at[dst, p], zs.at[ss, c], zr.at[slot, c], wide=who) for c, p in enumerate(z_part)]

    out_away = row_of(pk.at[0], 2, 0, 2, mate)
    out_home = row_of(pk.at[1], 3, 1, 3, mate)
    in_away = row_of(pk.at[0], 0, 0, 0, over)
    in_next = row_of(kbuf.at[2], 1, 1, 1, over)
    on_near = row_of(kbuf.at[0], 0, 2, 0, mate)
    on_far = row_of(kbuf.at[1], 1, 3, 1, mate)

    def tag_of(src, dst, ss, who):
        return send(src, kmeta.at[dst], zms.at[ss], zmr.at[dst], wide=who)

    t_out_away = tag_of(pm.at[0], 2, 0, mate)
    t_out_home = tag_of(pm.at[1], 3, 1, mate)
    t_in_away = tag_of(pm.at[0], 0, 0, over)
    t_in_next = tag_of(kmeta.at[2], 1, 1, over)
    t_on_near = tag_of(kmeta.at[0], 0, 2, mate)
    t_on_far = tag_of(kmeta.at[1], 1, 3, mate)

    @pl.when(outer)
    def _():
        t_out_away.start()
        t_out_home.start()
        for c in out_away + out_home:
            c.start()

    @pl.when(inner)
    def _():
        t_in_away.start()
        for c in in_away:
            c.start()

    cc.wait_recv()
    uq[1] = normed(qraw.at[0])
    own_part(1)

    @pl.when(inner)
    def _():
        t_out_away.wait_recv()
        t_in_next.start()
        t_in_away.wait_recv()
        t_on_near.start()

    for c in range(CHUNKS):
        xc[c].wait_recv()
        fc[c].start()

        @pl.when(inner)
        def _():
            out_away[c].wait_recv()
            in_next[c].start()
            in_away[c].wait_recv()
            on_near[c].start()

    uq[2] = normed(qraw.at[1])
    own_part(2)

    @pl.when(inner)
    def _():
        t_in_next.wait_recv()
        t_on_far.start()
        in_next[0].wait_recv()
        on_far[0].start()

    for c in fc:
        c.wait_recv()
    uq[3] = normed(qraw.at[2])
    own_part(3)

    def met_by(slot, ready=None):
        k_cl = tall(kmeta[slot][0:1], rows)
        k_od = tall(kmeta[slot][1:2], rows)
        quarter = half // 2
        cols = []
        for b in range(2):
            if ready is not None:
                for c in ready[b * CHUNKS // 2:(b + 1) * CHUNKS // 2]:
                    c.wait_recv()
            span = slice(b * quarter, (b + 1) * quarter)
            keys = kbuf[slot, span]
            col = jnp.full((quarter, rows), -1.0, f32)
            for j in range(4):
                q_cl, q_od = asked(j)
                same = jnp.where(k_cl[span] == q_cl, pair_inner(keys, uq[j]), -1.0)
                before = k_od[span] < q_od
                racc[j] = jnp.maximum(racc[j], jnp.max(jnp.where(before, same, -1.0), axis=0, keepdims=True))
                col = jnp.maximum(col, jnp.where(before, -1.0, same))
            cols.append(col)
        cacc[slot] = jnp.max(jnp.concatenate(cols, axis=0).T, axis=0, keepdims=True)

    def back(slot, dst, who):
        return send(cacc.at[slot], cres.at[dst], ts.at[slot], tr.at[dst], wide=who)

    b_in = [back(0, 0, over), back(1, 0, over_mate), back(2, 2, mate), back(3, 3, mate)]
    b_out = [back(0, 1, over_mate), back(1, 1, over)]

    @pl.when(inner)
    def _():
        in_next[1].wait_recv()
        on_far[1].start()
        met_by(0)
        b_in[0].start()
        for c in range(2, CHUNKS):
            in_next[c].wait_recv()
            on_far[c].start()
        met_by(1)
        b_in[1].start()
        t_out_home.wait_recv()
        for c in out_home:
            c.wait_recv()
        met_by(2)
        b_in[2].start()
        met_by(3)
        b_in[3].start()

    @pl.when(outer)
    def _():
        t_on_near.wait_recv()
        for c in on_near:
            c.wait_recv()
        met_by(0)
        b_out[0].start()
        t_on_far.wait_recv()
        met_by(1, on_far)
        b_out[1].start()

    rowb = [send(racc.at[j + 1], rres.at[j], rs.at[j], rr.at[j], narrow=peers[j]) for j in range(3)]
    for c in rowb:
        c.start()
    for c in rowb:
        c.wait_recv()
    b_in[0].wait_recv()
    b_out[0].wait_recv()
    cfull[:, :half] = jnp.maximum(cres[0], cres[1])
    cfull[:, half:] = jnp.full((1, half), -1.0, f32)

    @pl.when(outer)
    def _():
        b_in[2].wait_recv()
        b_in[3].wait_recv()
        cfull[:, :half] = jnp.maximum(cfull[:, :half], cres[2])
        cfull[:, half:] = cres[3]

    mine = jnp.where(deep.astype(f32) == target[...], tall(cfull[...], rows), -1.0)
    best = jnp.maximum(jnp.maximum(racc[0], rres[0]), jnp.maximum(rres[1], rres[2]))
    out[...] = jnp.maximum(best, jnp.max(mine, axis=0, keepdims=True))

    @pl.when(outer)
    def _():
        for c in [t_out_away, t_out_home] + out_away + out_home + b_out:
            c.wait_send()

    @pl.when(inner)
    def _():
        for c in [t_in_away, t_in_next, t_on_near, t_on_far] + in_away + in_next + on_near + on_far + b_in:
            c.wait_send()

    for c in ids + orders + xc + [cc] + fc + rowb:
        c.wait_send()


def per_device_meet(embeddings, cluster_id, order_index):
    rows, width = embeddings.shape
    half = rows // 2
    dma = pltpu.SemaphoreType.DMA
    vmem = pl.BlockSpec(memory_space=pltpu.VMEM)
    line = lambda k, m: pltpu.VMEM((k, 1, m), jnp.float32)
    block = lambda k, m: pltpu.VMEM((k, m, width), jnp.bfloat16)
    found = pl.pallas_call(
        meet_kernel,
        out_shape=jax.ShapeDtypeStruct((1, rows), jnp.float32),
        in_specs=[pl.BlockSpec(memory_space=pl.ANY), vmem, vmem],
        out_specs=vmem,
        scratch_shapes=[
            pltpu.VMEM((rows, width), jnp.bfloat16), dma, block(3, rows), block(4, rows),
            pltpu.VMEM((SIDE * SIDE, 1, rows), jnp.int32), pltpu.VMEM((3, 1, rows), jnp.int32),
            block(2, half), pltpu.VMEM((2, 2, half), jnp.float32),
            block(4, half), pltpu.VMEM((4, 2, half), jnp.float32),
            pltpu.VMEM((1, rows), jnp.float32),
            line(4, rows), line(3, rows), line(4, half), line(4, half), pltpu.VMEM((1, rows), jnp.float32),
            dma((CHUNKS,)), dma((CHUNKS,)), dma((CHUNKS,)), dma((CHUNKS,)), dma, dma,
            dma((SIDE * SIDE,)), dma((SIDE * SIDE,)), dma((3,)), dma((3,)),
            dma((4, CHUNKS)), dma((4, CHUNKS)), dma((4,)), dma((4,)),
            dma((3,)), dma((3,)), dma((4,)), dma((4,)),
        ],
        compiler_params=pltpu.CompilerParams(collective_id=0, has_side_effects=True),
    )(embeddings, cluster_id.reshape(1, rows), order_index.reshape(1, rows))
    return jnp.maximum(found.reshape(rows), -1.0)


def solution(mesh):
    meet = mesh.shape["wide"] == SIDE and mesh.shape["narrow"] == SIDE
    return jax.shard_map(
        per_device_meet if meet else per_device,
        mesh=mesh,
        in_specs=(
            P(("parts", "wide", "narrow"), None),
            P(("parts", "wide", "narrow")),
            P(("parts", "wide", "narrow")),
        ),
        out_specs=P(("parts", "wide", "narrow")),
        check_vma=False,
    )
```
